512 devices in a mesh: layer: 32 (over x, z_lo), dp: 16 (over y, z_hi, core).
Axes of the slice: x: 4, y: 4, z: 16 (z_hi: 2, z_lo: 8; z = z_hi * 8 + z_lo), core: 2. Of those that a mesh axis runs over, the one named last changes fastest.
Arguments:
- activations: bfloat16 [32, 10240, 2048], P('layer', 'dp'), may hold values from -6 to 6
- out_grads: bfloat16 [32, 10240, 512], P('layer', 'dp'), may hold values from -0.059814453 to 0.059814453
- a_inverse: bfloat16 [32, 2048, 2048], P('layer', 'dp'), may hold values from -1 to 3, as said below
- s_inverse: bfloat16 [32, 512, 512], P('layer'), may hold values from -1 to 3, as said below
- in_decay: float32 [32, 2048], P('layer', 'dp'), may hold values from 0 to 1
- out_decay: float32 [32, 512], P('layer'), may hold values from 0 to 1
Outputs:
- direction: bfloat16 [32, 2048, 512], P('layer', 'dp')
The draws below stay inside these ranges and needn't reach their ends.
Inputs may be any that keep to these rules, and one draw needn't show every extreme that they name: `a_inverse`: each layer's matrix is a positive diagonal plus dense small entries. `s_inverse`: each layer's matrix is a positive diagonal plus dense small entries.
All inputs are finite; a program needn't handle non-finite values.
Results may differ from the reference program's by a relative error of at most 0.0036.
Values may be sent and summed in bfloat16 or wider, within the bound.
A program may use at most 64 MiB of HBM per device.

```python
import math
import jax
import jax.numpy as jnp
from jax import lax

DIN = 2048
DOUT = 512
LAYER_TOTAL = 32
TOKENS = 10240


def dense_inverse(key, order):
    diag_key = jax.random.fold_in(key, 11)
    noise_key = jax.random.fold_in(key, 12)
    diagonal = jax.random.uniform(diag_key, (LAYER_TOTAL, order), jnp.float32, 0.5, 2.0)
    noise = jnp.clip(jax.random.normal(noise_key, (LAYER_TOTAL, order, order), jnp.float32), -5.0, 5.0)
    spread = 0.5 / math.sqrt(order)
    return noise * spread + diagonal[:, :, None] * jnp.eye(order, dtype=jnp.float32)


def draw_a_inverse(key, part):
    return dense_inverse(jax.random.fold_in(key, 101), DIN).astype(jnp.bfloat16)


def draw_s_inverse(key, part):
    return dense_inverse(jax.random.fold_in(key, 202), DOUT).astype(jnp.bfloat16)


def decay_table(key, feature_width):
    flag_key = jax.random.fold_in(key, 21)
    slow_key = jax.random.fold_in(key, 22)
    fast_key = jax.random.fold_in(key, 23)
    jitter_key = jax.random.fold_in(key, 24)
    spike_key = jax.random.fold_in(key, 25)
    level_key = jax.random.fold_in(key, 26)
    share = 0.5
    slow = jax.random.uniform(flag_key, (feature_width,), jnp.float32) < share
    slow_rate = jnp.exp(-jax.random.uniform(slow_key, (feature_width,), jnp.float32) * math.log(10.0) / (2.0 * LAYER_TOTAL))
    fast_rate = jax.random.uniform(fast_key, (feature_width,), jnp.float32, 0.3, 0.6)
    base = jnp.where(slow, slow_rate, fast_rate)
    power = jax.random.uniform(jitter_key, (LAYER_TOTAL, feature_width), jnp.float32, 0.5, 1.5)
    table = base[None, :] ** power
    spike_layers = jax.random.randint(spike_key, (2,), 0, LAYER_TOTAL)
    spike_depth = jax.random.uniform(level_key, (2, feature_width), jnp.float32, 0.5, 0.8)
    layer_numbers = jnp.arange(LAYER_TOTAL)[:, None]
    multiplier = jnp.where(layer_numbers == spike_layers[0], spike_depth[0][None, :], 1.0)
    multiplier = multiplier * jnp.where(layer_numbers == spike_layers[1], spike_depth[1][None, :], 1.0)
    return table * multiplier


def draw_in_decay(key, part):
    return decay_table(jax.random.fold_in(key, 303), DIN)


def draw_out_decay(key, part):
    return decay_table(jax.random.fold_in(key, 404), DOUT)


def block_levels(stream_key, dims, shards, least, top_value):
    def one(axis_at, shards_of):
        steps = jax.random.uniform(jax.random.fold_in(jax.random.fold_in(stream_key, 6), axis_at), (shards_of,), jnp.float32, least / len(shards), top_value / len(shards))
        return jnp.repeat(jnp.exp(steps), dims[axis_at] // shards_of).reshape((-1,) + (1,) * (len(dims) - axis_at - 1))

    loudness = one(*shards[0])
    for cut in shards[1:]:
        loudness = loudness * one(*cut)
    return loudness


def normal_values(rng, dims, scale, bound, split=(), kind=jnp.bfloat16):
    result = jax.random.normal(rng, dims, jnp.float32) * scale
    if len(split) > 0:
        result = block_levels(rng, dims, split, -0.22, 0.18) * result
    return jnp.clip(result, min=-bound, max=bound).astype(kind)


def setup_inputs(seed: int = 0) -> dict:
    key_of = jax.random.split(jax.random.key(seed), 7)
    return {
        "activations": normal_values(key_of[0], (LAYER_TOTAL, TOKENS, DIN), 1.0, 6.0, ((0, 32), (1, 16))),
        "out_grads": normal_values(key_of[1], (LAYER_TOTAL, TOKENS, DOUT), 0.01, 0.059814453, ((0, 32), (1, 16))),
        "a_inverse": draw_a_inverse(jax.random.fold_in(key_of[6], 71), 0),
        "s_inverse": draw_s_inverse(jax.random.fold_in(key_of[6], 71), 0),
        "in_decay": draw_in_decay(jax.random.fold_in(key_of[6], 71), 0),
        "out_decay": draw_out_decay(jax.random.fold_in(key_of[6], 71), 0),
    }


def layer_grad(pair):
    return lax.dot_general(pair[0], pair[1], (((0,), (0,)), ((), ())), preferred_element_type=jnp.float32)

def reference(activations, out_grads, a_inverse, s_inverse, in_decay, out_decay):
    grad = lax.map(layer_grad, (activations, out_grads))
    coupling = in_decay[:, :, None] * out_decay[:, None, :]

    def up_step(carry, pair):
        value = pair[0] + pair[1] * carry
        return (value, value)
    start = jnp.zeros((DIN, DOUT), jnp.float32)
    carry_end, upper = lax.scan(up_step, start, (grad, coupling), reverse=True)

    def side_s(pair):
        return jnp.dot(pair[0].astype(jnp.bfloat16), pair[1], preferred_element_type=jnp.float32).astype(jnp.bfloat16)
    s_applied = lax.map(side_s, (upper, s_inverse))

    def side_a(pair):
        return jnp.dot(pair[0], pair[1], preferred_element_type=jnp.float32)
    solved = lax.map(side_a, (a_inverse, s_applied))

    def down_step(state, pair):
        value = pair[0] + state
        return (pair[1] * value, value)
    state_end, lower = lax.scan(down_step, start, (solved, coupling))
    return lower.astype(jnp.bfloat16)
```

```python
import jax
import jax.numpy as jnp
from jax import lax
from jax.experimental import pallas as pl
from jax.experimental.pallas import tpu as pltpu
from jax.sharding import PartitionSpec as P

MESH = pl.DeviceIdType.MESH
BF16 = jnp.bfloat16
F32 = jnp.float32

LAYERS, XS, ZL, YS, ZS = 32, 4, 8, 4, 16
TOK, DIN, DOUT, ROWS = 640, 2048, 512, 128


def off16(i):
    half = lax.div(i + 1, 2)
    return 8 + half * (1 - 2 * lax.rem(i, 2))


def off8(i):
    half = lax.div(i + 1, 2)
    return 4 + half * (1 - 2 * lax.rem(i, 2))


def kernel(
    acts, og, ainv, sinv, ind, outd, out,
    a_v, og_v, ai_v, si_v, ps, pr, v, so, sd, sf, ro, rd, rf, t, r, dk, dks, it, cpl, u, ul, sa, xs, rx, dd,
    ld_a, ld_o, ld_ai, ld_si, pair_s, pair_r, y_s, yo_r, yd_r, yf_r, dk_s, dk_r, r_s, r_r, u_s, u_r,
    sa_s, sa_r, sp_s, sp_r, x_s, x_r, d_s, d_r,
):
    lay = lax.axis_index("layer")
    dp = lax.axis_index("dp")
    x, zl = lax.div(lay, ZL), lax.rem(lay, ZL)
    y, zh, c = lax.div(dp, 4), lax.rem(lax.div(dp, 2), 2), lax.rem(dp, 2)
    z = zh * ZL + zl
    y1 = y + 1 - 2 * lax.rem(y, 2)
    y2 = lax.rem(y + 2, YS)
    y3 = YS - 1 - y
    oc = 1 - c
    me = zh * LAYERS + lay

    def at(layer, yy, hh, cc):
        return {"layer": layer, "dp": yy * 4 + hh * 2 + cc}

    partner = at(lay, y, zh, oc)
    near1 = at(lay, y1, zh, c)
    near3 = at(lay, y3, zh, c)

    barrier = pltpu.get_barrier_semaphore()

    def greet(i, carry):
        q = lax.rem(me + i, 2 * LAYERS)
        pl.semaphore_signal(
            barrier, inc=1, device_id=at(lax.rem(q, LAYERS), y, lax.div(q, LAYERS), c), device_id_type=MESH
        )
        return carry

    lax.fori_loop(1, 2 * LAYERS, greet, 0)
    for dev in (partner, near1, near3):
        pl.semaphore_signal(barrier, inc=1, device_id=dev, device_id_type=MESH)

    loads = []
    for jr in range(4):
        src = pl.multiple_of(lax.rem(x + jr, 4) * 128, 128)
        cp = pltpu.make_async_copy(og.at[0, :, pl.ds(src, 128)], og_v.at[:, pl.ds(jr * 128, 128)], ld_o)
        cp.start()
    for ci, cc in ((0, oc), (1, c)):
        for k, yy in enumerate((y2, y1, y3, y)):
            for h in range(2):
                src = pl.multiple_of(yy * 512 + h * 256 + cc * 128, 128)
                pltpu.make_async_copy(
                    acts.at[0, :, pl.ds(src, 128)], a_v.at[k, ci, :, pl.ds(h * 128, 128)], ld_a.at[k, ci]
                ).start()
    for ci, cc in ((0, oc), (1, c)):
        for k, yy in enumerate((y2, y1, y3, y)):
            for h in range(2):
                src = pl.multiple_of(yy * 512 + h * 256 + cc * 128, 128)
                pltpu.make_async_copy(
                    ainv.at[0, :, pl.ds(src, 128)], ai_v.at[k, ci, :, pl.ds(h * 128, 128)], ld_ai
                ).start()
    pltpu.make_async_copy(sinv.at[0], si_v, ld_si).start()

    dk[0:1, :] = ind[...]
    for j in range(4):
        dk[1 + j : 2 + j, :] = outd[0:1, j * 128 : (j + 1) * 128]

    pltpu.make_async_copy(og_v, og_v, ld_o).wait()

    def product(k, ci):
        pltpu.make_async_copy(a_v.at[k, ci], a_v.at[k, ci], ld_a.at[k, ci]).wait()
        return lax.dot_general(
            a_v[k, ci], og_v[...], (((0,), (0,)), ((), ())), preferred_element_type=F32
        )

    for k in range(4):
        g = product(k, 0)
        for j in range(4):
            ps[k, j] = g[:, j * 128 : (j + 1) * 128]
    for k in range(4):
        g = product(k, 1)
        for j in range(4):
            v[k, j] = g[:, j * 128 : (j + 1) * 128]

    pl.semaphore_wait(barrier, 2 * LAYERS - 1 + 3)

    def send(src, dst, ssem, rsem, dev):
        cp = pltpu.make_async_remote_copy(
            src_ref=src, dst_ref=dst, send_sem=ssem, recv_sem=rsem, device_id=dev, device_id_type=MESH
        )
        cp.start()

    def wait(ref, sem):
        pltpu.make_async_copy(ref, ref, sem).wait()

    for k in range(4):
        send(ps.at[k], pr.at[k], pair_s, pair_r.at[k], partner)

    def send_decay(i, carry):
        q = lax.rem(lay + i, LAYERS)
        send(dk, dks.at[lay], dk_s, dk_r, at(q, y, zh, c))
        return carry

    lax.fori_loop(1, LAYERS, send_decay, 0)
    pltpu.make_async_copy(dk, dks.at[lay], dk_r).start()

    first = (near1, near1, near3, near3)
    second = (near3, near3, near1, near1)
    k_first = (1, 1, 2, 2)
    k_second = (2, 2, 1, 1)
    wait(pr.at[0], pair_r.at[0])
    for j in (0, 2, 1, 3):
        so[j] = (v[0, j] + pr[0, j]).astype(BF16)
        send(so.at[j], ro.at[j], y_s, yo_r.at[j], first[j])
    wait(pr.at[1], pair_r.at[1])
    wait(pr.at[2], pair_r.at[2])
    for j in (0, 2, 1, 3):
        k = k_first[j]
        sd[j] = (v[k, j] + pr[k, j]).astype(BF16)
        send(sd.at[j], rd.at[j], y_s, yd_r.at[j], first[j])
    for j in (0, 2, 1, 3):
        k = k_second[j]
        wait(ro.at[j], yo_r.at[j])
        sf[j] = v[k, j] + pr[k, j] + ro[j].astype(F32)
        send(sf.at[j], rf.at[j], y_s, yf_r.at[j], second[j])
    wait(pr.at[3], pair_r.at[3])
    for j in (0, 2, 1, 3):
        wait(rd.at[j], yd_r.at[j])
        wait(rf.at[j], yf_r.at[j])
        total = v[3, j] + pr[3, j] + rd[j].astype(F32) + rf[j]
        t[j] = total.astype(BF16).reshape(ZS, 16, 128)
        xx = lax.rem(x + j, XS)

        def send_tile(i, carry, j=j, xx=xx):
            zz = lax.rem(z + off16(i), ZS)
            dev = at(xx * ZL + lax.rem(zz, ZL), y, lax.div(zz, ZL), c)
            send(t.at[j, zz], r.at[me], r_s, r_r, dev)
            return carry

        lax.fori_loop(0, 15 if j == 0 else 16, send_tile, 0)
        if j == 0:
            pltpu.make_async_copy(t.at[0, z], r.at[me], r_r).start()

    wait(dks, dk_r)
    rates = dks[:, 0, :]
    it[...] = jnp.concatenate([rates, jnp.zeros((128 - LAYERS, 128), F32)], axis=0).T
    mine = it[pl.ds(pl.multiple_of(zl * 16, 16), 16), :]
    for l in range(LAYERS):
        cpl[l] = mine[:, l : l + 1] * dks[l, pl.ds(1 + x, 1), :]

    wait(r, r_r)
    state = None
    for l in reversed(range(LAYERS)):
        grad = r[l].astype(F32) + r[LAYERS + l].astype(F32)
        state = grad if state is None else grad + cpl[l] * state
        u[l] = state.astype(BF16)

    spot = (pl.ds(pl.multiple_of(z * 16, 16), 16), pl.ds(pl.multiple_of(x * 128, 128), 128))
    for j in range(4):
        xx = lax.rem(x + j, XS)

        def send_upper(i, carry, j=j, xx=xx):
            zz = lax.rem(z + off16(i), ZS)
            ll = xx * ZL + lax.rem(zz, ZL)
            send(u.at[ll], ul.at[spot], u_s, u_r, at(ll, y, lax.div(zz, ZL), c))
            return carry

        lax.fori_loop(0, 15 if j == 0 else 16, send_upper, 0)
    pltpu.make_async_copy(u.at[lay], ul.at[spot], u_r).start()

    wait(si_v, ld_si)
    wait(ul, u_r)
    sa[3, 1] = jnp.dot(ul[...], si_v[...], preferred_element_type=F32).astype(BF16)

    half = (pl.ds(0, 128), pl.ds(128, 128))
    own = sa.at[3, 1]
    send(own.at[half[0]], sa.at[1, 1, half[0]], sa_s, sa_r.at[0], near1)
    send(own.at[half[1]], sa.at[2, 1, half[1]], sa_s, sa_r.at[1], near3)
    send(own.at[half[1]], sa.at[1, 1, half[1]], sa_s, sa_r.at[2], near1)
    send(own.at[half[0]], sa.at[2, 1, half[0]], sa_s, sa_r.at[3], near3)
    send(own, sa.at[3, 0], sp_s, sp_r.at[3], partner)

    wait(ai_v, ld_ai)
    acc = jnp.dot(ai_v[3, 1], sa[3, 1], preferred_element_type=F32)
    wait(sa.at[1, 1, half[0]], sa_r.at[0])
    send(sa.at[1, 1, half[0]], sa.at[0, 1, half[0]], sa_s, sa_r.at[4], near3)
    wait(sa.at[2, 1, half[1]], sa_r.at[1])
    send(sa.at[2, 1, half[1]], sa.at[0, 1, half[1]], sa_s, sa_r.at[5], near1)
    wait(sa.at[3, 0], sp_r.at[3])
    acc += jnp.dot(ai_v[3, 0], sa[3, 0], preferred_element_type=F32)
    wait(sa.at[1, 1, half[1]], sa_r.at[2])
    send(sa.at[1, 1], sa.at[1, 0], sp_s, sp_r.at[1], partner)
    wait(sa.at[2, 1, half[0]], sa_r.at[3])
    send(sa.at[2, 1], sa.at[2, 0], sp_s, sp_r.at[2], partner)
    acc += jnp.dot(ai_v[1, 1], sa[1, 1], preferred_element_type=F32)
    acc += jnp.dot(ai_v[2, 1], sa[2, 1], preferred_element_type=F32)
    wait(sa.at[1, 0], sp_r.at[1])
    acc += jnp.dot(ai_v[1, 0], sa[1, 0], preferred_element_type=F32)
    wait(sa.at[2, 0], sp_r.at[2])
    acc += jnp.dot(ai_v[2, 0], sa[2, 0], preferred_element_type=F32)
    wait(sa.at[0, 1, half[0]], sa_r.at[4])
    wait(sa.at[0, 1, half[1]], sa_r.at[5])
    send(sa.at[0, 1], sa.at[0, 0], sp_s, sp_r.at[0], partner)
    acc += jnp.dot(ai_v[0, 1], sa[0, 1], preferred_element_type=F32)
    wait(sa.at[0, 0], sp_r.at[0])
    acc += jnp.dot(ai_v[0, 0], sa[0, 0], preferred_element_type=F32)

    for j in range(4):
        xs[j] = acc[:, j * 128 : (j + 1) * 128].astype(BF16).reshape(ZL, 16, 128)
    for j in range(4):
        xx = lax.rem(x + j, XS)

        def send_solved(i, carry, xx=xx):
            zz = lax.rem(zl + off8(i), ZL)
            send(xs.at[xx, zz], rx.at[lay], x_s, x_r, at(xx * ZL + zz, y, zh, c))
            return carry

        lax.fori_loop(0, 7 if j == 0 else 8, send_solved, 0)
    pltpu.make_async_copy(xs.at[x, zl], rx.at[lay], x_r).start()

    wait(rx, x_r)
    state = None
    for l in range(LAYERS):
        solved = rx[l].astype(F32)
        state = solved if state is None else solved + cpl[l - 1] * state
        dd[l] = state.astype(BF16)

    place = (0, pl.ds(pl.multiple_of(zl * 16, 16), 16), pl.ds(pl.multiple_of(x * 128, 128), 128))
    for j in range(4):
        xx = lax.rem(x + j, XS)

        def send_lower(i, carry, xx=xx):
            zz = lax.rem(zl + off8(i), ZL)
            ll = xx * ZL + zz
            send(dd.at[ll], out.at[place], d_s, d_r, at(ll, y, zh, c))
            return carry

        lax.fori_loop(0, 7 if j == 0 else 8, send_lower, 0)
    pltpu.make_async_copy(dd.at[lay], out.at[place], d_r).start()

    wait(ps, pair_s)
    wait(so, y_s)
    wait(sd, y_s)
    wait(sf, y_s)
    wait(dks.at[pl.ds(0, LAYERS - 1)], dk_s)
    wait(r.at[pl.ds(0, 2 * LAYERS - 1)], r_s)
    wait(r.at[pl.ds(0, 2 * LAYERS - 1)], u_s)
    wait(sa.at[pl.ds(0, 1), 0], sa_s)
    wait(sa.at[pl.ds(0, 1), 0], sa_s)
    wait(sa.at[pl.ds(0, 1), 0], sa_s)
    wait(sa.at[:, 0], sp_s)
    wait(rx.at[pl.ds(0, LAYERS - 1)], x_s)
    wait(rx.at[pl.ds(0, LAYERS - 1)], d_s)
    wait(out, d_r)


def shards(activations, out_grads, a_inverse, s_inverse, in_decay, out_decay):
    vm = pltpu.VMEM
    dma = pltpu.SemaphoreType.DMA
    anywhere = pl.BlockSpec(memory_space=pl.ANY)
    inside = pl.BlockSpec(memory_space=pltpu.VMEM)
    unit = (4, 256, 128)
    scratch = [
        vm((4, 2, TOK, 256), BF16),
        vm((TOK, DOUT), BF16),
        vm((4, 2, ROWS, 256), BF16),
        vm((DOUT, DOUT), BF16),
        vm((4, 4, 256, 128), F32),
        vm((4, 4, 256, 128), F32),
        vm((4, 4, 256, 128), F32),
        vm(unit, BF16), vm(unit, BF16), vm(unit, F32),
        vm(unit, BF16), vm(unit, BF16), vm(unit, F32),
        vm((4, ZS, 16, 128), BF16),
        vm((2 * LAYERS, 16, 128), BF16),
        vm((8, 128), F32),
        vm((LAYERS, 8, 128), F32),
        vm((128, 128), F32),
        vm((LAYERS, 16, 128), F32),
        vm((LAYERS, 16, 128), BF16),
        vm((256, DOUT), BF16),
        vm((4, 2, 256, DOUT), BF16),
        vm((4, ZL, 16, 128), BF16),
        vm((LAYERS, 16, 128), BF16),
        vm((LAYERS, 16, 128), BF16),
        dma((4, 2)), dma(()), dma(()), dma(()),
        dma(()), dma((4,)),
        dma(()), dma((4,)), dma((4,)), dma((4,)),
        dma(()), dma(()),
        dma(()), dma(()),
        dma(()), dma(()),
        dma(()), dma((6,)),
        dma(()), dma((4,)),
        dma(()), dma(()),
        dma(()), dma(()),
    ]
    return pl.pallas_call(
        kernel,
        out_shape=jax.ShapeDtypeStruct((1, ROWS, DOUT), BF16),
        in_specs=[anywhere] * 4 + [inside] * 2,
        out_specs=inside,
        scratch_shapes=scratch,
        compiler_params=pltpu.CompilerParams(
            collective_id=0, has_side_effects=True, vmem_limit_bytes=48 * 1024 * 1024
        ),
    )(activations, out_grads, a_inverse, s_inverse, in_decay, out_decay)


def solution(mesh):
    placed = (
        P("layer", "dp", None),
        P("layer", "dp", None),
        P("layer", "dp", None),
        P("layer", None, None),
        P("layer", "dp"),
        P("layer", None),
    )
    return jax.shard_map(
        shards, mesh=mesh, in_specs=placed, out_specs=P("layer", "dp", None), check_vma=False
    )
```

```python
import jax
import jax.numpy as jnp
from jax import lax
from jax.experimental import pallas as pl
from jax.experimental.pallas import tpu as pltpu
from jax.sharding import PartitionSpec as P

MESH = pl.DeviceIdType.MESH
BF16 = jnp.bfloat16
F32 = jnp.float32

LAYERS, XS, ZL, YS, ZS = 32, 4, 8, 4, 16
TOK, DIN, DOUT, ROWS = 640, 2048, 512, 128


def off16(i):
    half = lax.div(i + 1, 2)
    return 8 + half * (1 - 2 * lax.rem(i, 2))


def off8(i):
    half = lax.div(i + 1, 2)
    return 4 + half * (1 - 2 * lax.rem(i, 2))


def kernel(
    acts, og, ainv, sinv, ind, outd, out,
    a_v, og_v, og_t, ai_v, si_v, ind_v, outd_v, g, pr, so, sd, sf, ro, rd, rf, t, r, dk, dks, it, cpl, u, ul, sa, xs, rx, dd,
    ld_a, ld_o, ld_ai, ld_si, ld_d, round_s, pair_s, pair_r, y_s, yo_r, yd_r, yf_r, dk_s, dk_r, r_s, r_r, u_s, u_r,
    sa_s, sa_r, sp_s, sp_r, x_s, x_r, d_s, d_r,
):
    lay = lax.axis_index("layer")
    dp = lax.axis_index("dp")
    x, zl = lax.div(lay, ZL), lax.rem(lay, ZL)
    y, zh, c = lax.div(dp, 4), lax.rem(lax.div(dp, 2), 2), lax.rem(dp, 2)
    z = zh * ZL + zl
    y1 = y + 1 - 2 * lax.rem(y, 2)
    y2 = lax.rem(y + 2, YS)
    y3 = YS - 1 - y
    oc = 1 - c
    me = zh * LAYERS + lay

    def at(layer, yy, hh, cc):
        return {"layer": layer, "dp": yy * 4 + hh * 2 + cc}

    partner = at(lay, y, zh, oc)
    near1 = at(lay, y1, zh, c)
    near3 = at(lay, y3, zh, c)

    def send(src, dst, ssem, rsem, dev):
        pltpu.make_async_remote_copy(
            src_ref=src, dst_ref=dst, send_sem=ssem, recv_sem=rsem, device_id=dev, device_id_type=MESH
        ).start()

    def wait(ref, sem):
        pltpu.make_async_copy(ref, ref, sem).wait()

    def signal(sem, dev):
        pl.semaphore_signal(sem, inc=1, device_id=dev, device_id_type=MESH)

    def along_z(step):
        zz = lax.rem(z + step + ZS, ZS)
        return at(x * ZL + lax.rem(zz, ZL), y, lax.div(zz, ZL), c)

    def along_x(step):
        return at(lax.rem(x + step, XS) * ZL + zl, y, zh, c)

    barrier = pltpu.get_barrier_semaphore()
    for dev in (partner, near1, near3, along_z(1), along_z(-1), along_x(1), along_x(2), along_x(3)):
        signal(barrier, dev)

    for jr in range(4):
        src = pl.multiple_of(lax.rem(x + jr, 4) * 128, 128)
        pltpu.make_async_copy(og.at[0, :, pl.ds(src, 128)], og_v.at[:, pl.ds(jr * 128, 128)], ld_o).start()
    for i in range(5):
        rows = pl.ds(i * 128, 128)
        pltpu.make_async_copy(acts.at[0, rows], a_v.at[rows], ld_a).start()
    pltpu.make_async_copy(ind, ind_v, ld_d.at[0]).start()
    pltpu.make_async_copy(outd, outd_v, ld_d.at[1]).start()
    for ci, cc in ((0, oc), (1, c)):
        for k, yy in enumerate((y2, y1, y3, y)):
            for h in range(2):
                src = pl.multiple_of(yy * 512 + h * 256 + cc * 128, 128)
                pltpu.make_async_copy(
                    ainv.at[0, :, pl.ds(src, 128)], ai_v.at[k, ci, :, pl.ds(h * 128, 128)], ld_ai
                ).start()
    pltpu.make_async_copy(sinv.at[0], si_v, ld_si).start()

    wait(og_v, ld_o)
    og_t[...] = og_v[...].T
    wait(a_v, ld_a)

    def product(k, yy):
        for h in range(2):
            src = pl.multiple_of(yy * 512 + h * 256, 256)
            part = jnp.dot(og_t[...], a_v[:, pl.ds(src, 256)], preferred_element_type=F32)
            for cc in range(2):
                for j in range(4):
                    g[cc, k, j, h] = part[j * 128 : (j + 1) * 128, cc * 128 : (cc + 1) * 128]

    product(0, y2)
    pl.semaphore_wait(barrier, 8)
    send(g.at[oc, 0], pr.at[0], pair_s, pair_r.at[0], partner)
    signal(round_s.at[0], along_z(1))
    signal(round_s.at[0], along_z(-1))
    product(1, y1)
    send(g.at[oc, 1], pr.at[1], pair_s, pair_r.at[1], partner)
    product(2, y3)
    send(g.at[oc, 2], pr.at[2], pair_s, pair_r.at[2], partner)
    pl.semaphore_wait(round_s.at[0], 2)
    signal(round_s.at[1], along_z(2))
    signal(round_s.at[1], along_z(-2))
    product(3, y)
    send(g.at[oc, 3], pr.at[3], pair_s, pair_r.at[3], partner)

    wait(ind_v, ld_d.at[0])
    wait(outd_v, ld_d.at[1])
    dk[...] = jnp.zeros_like(dk)
    dk[0:1, :] = ind_v[...]
    for j in range(4):
        dk[1 + j : 2 + j, :] = outd_v[0:1, j * 128 : (j + 1) * 128]

    first = (near1, near1, near3, near3)
    second = (near3, near3, near1, near1)
    k_first = (1, 1, 2, 2)
    k_second = (2, 2, 1, 1)
    wait(pr.at[0], pair_r.at[0])
    for j in (0, 2, 1, 3):
        so[j] = (g[c, 0, j] + pr[0, j]).astype(BF16)
        send(so.at[j], ro.at[j], y_s, yo_r.at[j], first[j])
    pl.semaphore_wait(round_s.at[1], 2)
    signal(round_s.at[2], along_z(4))
    signal(round_s.at[2], along_z(-4))
    wait(pr.at[1], pair_r.at[1])
    wait(pr.at[2], pair_r.at[2])
    for j in (0, 2, 1, 3):
        k = k_first[j]
        sd[j] = (g[c, k, j] + pr[k, j]).astype(BF16)
        send(sd.at[j], rd.at[j], y_s, yd_r.at[j], first[j])
    pl.semaphore_wait(round_s.at[2], 2)
    for step in range(1, XS):
        signal(round_s.at[3], along_x(step))
    for j in (0, 2, 1, 3):
        k = k_second[j]
        wait(ro.at[j], yo_r.at[j])
        sf[j] = g[c, k, j] + pr[k, j] + ro[j].astype(F32)
        send(sf.at[j], rf.at[j], y_s, yf_r.at[j], second[j])

    pl.semaphore_wait(round_s.at[3], XS - 1)

    def send_decay(i, carry):
        q = lax.rem(lay + i, LAYERS)
        send(dk, dks.at[lay], dk_s, dk_r, at(q, y, zh, c))
        return carry

    lax.fori_loop(1, LAYERS, send_decay, 0)
    pltpu.make_async_copy(dk, dks.at[lay], dk_r).start()

    wait(pr.at[3], pair_r.at[3])
    for j in (0, 2, 1, 3):
        wait(rd.at[j], yd_r.at[j])
        wait(rf.at[j], yf_r.at[j])
        total = g[c, 3, j] + pr[3, j] + rd[j].astype(F32) + rf[j]
        for h in range(2):
            t[j, h * ZL : (h + 1) * ZL] = total[h].T.astype(BF16).reshape(ZL, 16, 128)
        xx = lax.rem(x + j, XS)

        def send_tile(i, carry, j=j, xx=xx):
            zz = lax.rem(z + off16(i), ZS)
            dev = at(xx * ZL + lax.rem(zz, ZL), y, lax.div(zz, ZL), c)
            send(t.at[j, zz], r.at[me], r_s, r_r, dev)
            return carry

        lax.fori_loop(0, 15 if j == 0 else 16, send_tile, 0)
        if j == 0:
            pltpu.make_async_copy(t.at[0, z], r.at[me], r_r).start()

    wait(dks, dk_r)
    rates = dks[:, 0, :]
    it[...] = jnp.concatenate([rates, jnp.zeros((128 - LAYERS, 128), F32)], axis=0).T
    mine = it[pl.ds(pl.multiple_of(zl * 16, 16), 16), :]
    for l in range(LAYERS):
        cpl[l] = mine[:, l : l + 1] * dks[l, pl.ds(1 + x, 1), :]

    wait(r, r_r)
    state = None
    for l in reversed(range(LAYERS)):
        grad = r[l].astype(F32) + r[LAYERS + l].astype(F32)
        state = grad if state is None else grad + cpl[l] * state
        u[l] = state.astype(BF16)

    spot = (pl.ds(pl.multiple_of(z * 16, 16), 16), pl.ds(pl.multiple_of(x * 128, 128), 128))
    for j in range(4):
        xx = lax.rem(x + j, XS)

        def send_upper(i, carry, j=j, xx=xx):
            zz = lax.rem(z + off16(i), ZS)
            ll = xx * ZL + lax.rem(zz, ZL)
            send(u.at[ll], ul.at[spot], u_s, u_r, at(ll, y, lax.div(zz, ZL), c))
            return carry

        lax.fori_loop(0, 15 if j == 0 else 16, send_upper, 0)
    pltpu.make_async_copy(u.at[lay], ul.at[spot], u_r).start()

    wait(si_v, ld_si)
    wait(ul, u_r)
    sa[3, 1] = jnp.dot(ul[...], si_v[...], preferred_element_type=F32).astype(BF16)

    half = (pl.ds(0, 128), pl.ds(128, 128))
    own = sa.at[3, 1]
    send(own.at[half[0]], sa.at[1, 1, half[0]], sa_s, sa_r.at[0], near1)
    send(own.at[half[1]], sa.at[2, 1, half[1]], sa_s, sa_r.at[1], near3)
    send(own.at[half[1]], sa.at[1, 1, half[1]], sa_s, sa_r.at[2], near1)
    send(own.at[half[0]], sa.at[2, 1, half[0]], sa_s, sa_r.at[3], near3)
    send(own, sa.at[3, 0], sp_s, sp_r.at[3], partner)

    wait(ai_v, ld_ai)
    acc = jnp.dot(ai_v[3, 1], sa[3, 1], preferred_element_type=F32)
    wait(sa.at[1, 1, half[0]], sa_r.at[0])
    send(sa.at[1, 1, half[0]], sa.at[0, 1, half[0]], sa_s, sa_r.at[4], near3)
    wait(sa.at[2, 1, half[1]], sa_r.at[1])
    send(sa.at[2, 1, half[1]], sa.at[0, 1, half[1]], sa_s, sa_r.at[5], near1)
    wait(sa.at[3, 0], sp_r.at[3])
    acc += jnp.dot(ai_v[3, 0], sa[3, 0], preferred_element_type=F32)
    wait(sa.at[1, 1, half[1]], sa_r.at[2])
    send(sa.at[1, 1], sa.at[1, 0], sp_s, sp_r.at[1], partner)
    wait(sa.at[2, 1, half[0]], sa_r.at[3])
    send(sa.at[2, 1], sa.at[2, 0], sp_s, sp_r.at[2], partner)
    acc += jnp.dot(ai_v[1, 1], sa[1, 1], preferred_element_type=F32)
    acc += jnp.dot(ai_v[2, 1], sa[2, 1], preferred_element_type=F32)
    wait(sa.at[1, 0], sp_r.at[1])
    acc += jnp.dot(ai_v[1, 0], sa[1, 0], preferred_element_type=F32)
    wait(sa.at[2, 0], sp_r.at[2])
    acc += jnp.dot(ai_v[2, 0], sa[2, 0], preferred_element_type=F32)
    wait(sa.at[0, 1, half[0]], sa_r.at[4])
    wait(sa.at[0, 1, half[1]], sa_r.at[5])
    send(sa.at[0, 1], sa.at[0, 0], sp_s, sp_r.at[0], partner)
    acc += jnp.dot(ai_v[0, 1], sa[0, 1], preferred_element_type=F32)
    wait(sa.at[0, 0], sp_r.at[0])
    acc += jnp.dot(ai_v[0, 0], sa[0, 0], preferred_element_type=F32)

    for j in range(4):
        xs[j] = acc[:, j * 128 : (j + 1) * 128].astype(BF16).reshape(ZL, 16, 128)
    for j in range(4):
        xx = lax.rem(x + j, XS)

        def send_solved(i, carry, xx=xx):
            zz = lax.rem(zl + off8(i), ZL)
            send(xs.at[xx, zz], rx.at[lay], x_s, x_r, at(xx * ZL + zz, y, zh, c))
            return carry

        lax.fori_loop(0, 7 if j == 0 else 8, send_solved, 0)
    pltpu.make_async_copy(xs.at[x, zl], rx.at[lay], x_r).start()

    wait(rx, x_r)
    state = None
    for l in range(LAYERS):
        solved = rx[l].astype(F32)
        state = solved if state is None else solved + cpl[l - 1] * state
        dd[l] = state.astype(BF16)

    place = (0, pl.ds(pl.multiple_of(zl * 16, 16), 16), pl.ds(pl.multiple_of(x * 128, 128), 128))
    for j in range(4):
        xx = lax.rem(x + j, XS)

        def send_lower(i, carry, xx=xx):
            zz = lax.rem(zl + off8(i), ZL)
            ll = xx * ZL + zz
            send(dd.at[ll], out.at[place], d_s, d_r, at(ll, y, zh, c))
            return carry

        lax.fori_loop(0, 7 if j == 0 else 8, send_lower, 0)
    pltpu.make_async_copy(dd.at[lay], out.at[place], d_r).start()

    wait(pr, pair_s)
    wait(so, y_s)
    wait(sd, y_s)
    wait(sf, y_s)
    wait(dks.at[pl.ds(0, LAYERS - 1)], dk_s)
    wait(r.at[pl.ds(0, 2 * LAYERS - 1)], r_s)
    wait(r.at[pl.ds(0, 2 * LAYERS - 1)], u_s)
    wait(sa.at[pl.ds(0, 1), 0], sa_s)
    wait(sa.at[pl.ds(0, 1), 0], sa_s)
    wait(sa.at[pl.ds(0, 1), 0], sa_s)
    wait(sa.at[:, 0], sp_s)
    wait(rx.at[pl.ds(0, LAYERS - 1)], x_s)
    wait(rx.at[pl.ds(0, LAYERS - 1)], d_s)
    wait(out, d_r)


def shards(activations, out_grads, a_inverse, s_inverse, in_decay, out_decay):
    vm = pltpu.VMEM
    dma = pltpu.SemaphoreType.DMA
    outside = pl.BlockSpec(memory_space=pltpu.HBM)
    inside = pl.BlockSpec(memory_space=pltpu.VMEM)
    unit = (4, 2, 128, 128)
    scratch = [
        vm((TOK, DIN), BF16),
        vm((TOK, DOUT), BF16),
        vm((DOUT, TOK), BF16),
        vm((4, 2, ROWS, 256), BF16),
        vm((DOUT, DOUT), BF16),
        vm((1, ROWS), F32),
        vm((1, DOUT), F32),
        vm((2, 4, 4, 2, 128, 128), F32),
        vm((4, 4, 2, 128, 128), F32),
        vm(unit, BF16), vm(unit, BF16), vm(unit, F32),
        vm(unit, BF16), vm(unit, BF16), vm(unit, F32),
        vm((4, ZS, 16, 128), BF16),
        vm((2 * LAYERS, 16, 128), BF16),
        vm((8, 128), F32),
        vm((LAYERS, 8, 128), F32),
        vm((128, 128), F32),
        vm((LAYERS, 16, 128), F32),
        vm((LAYERS, 16, 128), BF16),
        vm((256, DOUT), BF16),
        vm((4, 2, 256, DOUT), BF16),
        vm((4, ZL, 16, 128), BF16),
        vm((LAYERS, 16, 128), BF16),
        vm((LAYERS, 16, 128), BF16),
        dma(()), dma(()), dma(()), dma(()), dma((2,)),
        pltpu.SemaphoreType.REGULAR((4,)),
        dma(()), dma((4,)),
        dma(()), dma((4,)), dma((4,)), dma((4,)),
        dma(()), dma(()),
        dma(()), dma(()),
        dma(()), dma(()),
        dma(()), dma((6,)),
        dma(()), dma((4,)),
        dma(()), dma(()),
        dma(()), dma(()),
    ]
    return pl.pallas_call(
        kernel,
        out_shape=jax.ShapeDtypeStruct((1, ROWS, DOUT), BF16),
        in_specs=[outside] * 6,
        out_specs=inside,
        scratch_shapes=scratch,
        compiler_params=pltpu.CompilerParams(
            collective_id=0, has_side_effects=True, vmem_limit_bytes=67043328
        ),
    )(activations, out_grads, a_inverse, s_inverse, in_decay, out_decay)


def solution(mesh):
    placed = (
        P("layer", "dp", None),
        P("layer", "dp", None),
        P("layer", "dp", None),
        P("layer", None, None),
        P("layer", "dp"),
        P("layer", None),
    )
    return jax.shard_map(
        shards, mesh=mesh, in_specs=placed, out_specs=P("layer", "dp", None), check_vma=False
    )
```

```python
import jax
import jax.numpy as jnp
from jax import lax
from jax.experimental import pallas as pl
from jax.experimental.pallas import tpu as pltpu
from jax.sharding import PartitionSpec as P

MESH = pl.DeviceIdType.MESH
BF16 = jnp.bfloat16
F32 = jnp.float32

LAYERS, XS, ZL, YS, ZS = 32, 4, 8, 4, 16
TOK, DIN, DOUT, ROWS = 640, 2048, 512, 128


def off8(i):
    half = lax.div(i + 1, 2)
    return 4 + half * (1 - 2 * lax.rem(i, 2))


def kernel(
    acts, og, ainv, sinv, ind, outd, out,
    a_v, og_v, og_t, ai_v, si_v, ind_v, outd_v, g, pr, so, sd, sf, ro, rd, rf, t, r, dk, dks, it, cpl, u, ul, sa, xs, rx, dd, ot,
    ld_a, ld_o, ld_ai, ld_si, ld_d, round_s, pair_s, pair_r, y_s, yo_r, yd_r, yf_r, dk_s, dk_r, r_s, r_r, u_s, u_r,
    sa_s, sa_r, sp_s, sp_r, x_s, x_r, d_s, d_r,
):
    lay = lax.axis_index("layer")
    dp = lax.axis_index("dp")
    x, zl = lax.div(lay, ZL), lax.rem(lay, ZL)
    y, zh, c = lax.div(dp, 4), lax.rem(lax.div(dp, 2), 2), lax.rem(dp, 2)
    z = zh * ZL + zl
    y1 = y + 1 - 2 * lax.rem(y, 2)
    y2 = lax.rem(y + 2, YS)
    y3 = YS - 1 - y
    oc = 1 - c
    me = zh * LAYERS + lay

    def at(layer, yy, hh, cc):
        return {"layer": layer, "dp": yy * 4 + hh * 2 + cc}

    partner = at(lay, y, zh, oc)
    near1 = at(lay, y1, zh, c)
    near2 = at(lay, y2, zh, c)
    near3 = at(lay, y3, zh, c)

    def send(src, dst, ssem, rsem, dev):
        pltpu.make_async_remote_copy(
            src_ref=src, dst_ref=dst, send_sem=ssem, recv_sem=rsem, device_id=dev, device_id_type=MESH
        ).start()

    def wait(ref, sem):
        pltpu.make_async_copy(ref, ref, sem).wait()

    def signal(sem, dev):
        pl.semaphore_signal(sem, inc=1, device_id=dev, device_id_type=MESH)

    def along_z(step):
        zz = lax.rem(z + step + ZS, ZS)
        return at(x * ZL + lax.rem(zz, ZL), y, lax.div(zz, ZL), c)

    def along_x(step):
        return at(lax.rem(x + step, XS) * ZL + zl, y, zh, c)

    barrier = pltpu.get_barrier_semaphore()
    for dev in (partner, near1, near2, near3, along_z(1), along_z(-1), along_x(1), along_x(2), along_x(3)):
        signal(barrier, dev)

    for jr in range(4):
        src = pl.multiple_of(lax.rem(x + jr, 4) * 128, 128)
        pltpu.make_async_copy(og.at[0, :, pl.ds(src, 128)], og_v.at[:, pl.ds(jr * 128, 128)], ld_o).start()
    for i in range(5):
        rows = pl.ds(i * 128, 128)
        pltpu.make_async_copy(acts.at[0, rows], a_v.at[rows], ld_a).start()
    pltpu.make_async_copy(ind, ind_v, ld_d.at[0]).start()
    pltpu.make_async_copy(outd, outd_v, ld_d.at[1]).start()
    for ci, cc in ((0, oc), (1, c)):
        for k, yy in enumerate((y2, y1, y3, y)):
            for h in range(2):
                src = pl.multiple_of(yy * 512 + h * 256 + cc * 128, 128)
                pltpu.make_async_copy(
                    ainv.at[0, :, pl.ds(src, 128)], ai_v.at[k, ci, :, pl.ds(h * 128, 128)], ld_ai
                ).start()
    pltpu.make_async_copy(sinv.at[0], si_v, ld_si).start()

    wait(og_v, ld_o)
    og_t[...] = og_v[...].T
    wait(a_v, ld_a)

    def product(k, yy):
        for h in range(2):
            src = pl.multiple_of(yy * 512 + h * 256, 256)
            part = jnp.dot(og_t[...], a_v[:, pl.ds(src, 256)], preferred_element_type=F32)
            for cc in range(2):
                for j in range(4):
                    g[cc, k, j, h] = part[j * 128 : (j + 1) * 128, cc * 128 : (cc + 1) * 128]

    product(0, y2)
    pl.semaphore_wait(barrier, 9)
    send(g.at[oc, 0], pr.at[0], pair_s, pair_r.at[0], partner)
    signal(round_s.at[0], along_z(1))
    signal(round_s.at[0], along_z(-1))
    product(1, y1)
    send(g.at[oc, 1], pr.at[1], pair_s, pair_r.at[1], partner)
    product(2, y3)
    send(g.at[oc, 2], pr.at[2], pair_s, pair_r.at[2], partner)
    pl.semaphore_wait(round_s.at[0], 2)
    signal(round_s.at[1], along_z(2))
    signal(round_s.at[1], along_z(-2))
    product(3, y)
    send(g.at[oc, 3], pr.at[3], pair_s, pair_r.at[3], partner)

    wait(ind_v, ld_d.at[0])
    wait(outd_v, ld_d.at[1])
    for j in range(XS):
        dk[j, 0:1, :] = ind_v[...]
        dk[j, 1:2, :] = outd_v[0:1, j * 128 : (j + 1) * 128]

    first = (near1, near1, near3, near3)
    second = (near3, near3, near1, near1)
    k_first = (1, 1, 2, 2)
    k_second = (2, 2, 1, 1)
    halves = (1 - zh, zh)
    chunks = (((0, 0), (2, 0)), ((0, 1), (2, 1)), ((1, 0), (3, 0)), ((1, 1), (3, 1)))

    def pair_sum(k, j, h):
        return g[c, k, j, halves[h]] + pr[k, j, halves[h]]

    def send_far(n):
        for j, h in chunks[n]:
            so[j, h] = pair_sum(0, j, h).astype(BF16)
            send(so.at[j, h], ro.at[j, h], y_s, yo_r.at[j, h], first[j])

    def send_first(n):
        for j, h in chunks[n]:
            sd[j, h] = pair_sum(k_first[j], j, h).astype(BF16)
            send(sd.at[j, h], rd.at[j, h], y_s, yd_r.at[j, h], first[j])

    def send_second(n):
        for j, h in chunks[n]:
            wait(ro.at[j, h], yo_r.at[j, h])
            sf[j, h] = pair_sum(k_second[j], j, h) + ro[j, h].astype(F32)
            send(sf.at[j, h], rf.at[j, h], y_s, yf_r.at[j, h], second[j])

    def send_tiles(n):
        for j, h in chunks[n]:
            wait(rd.at[j, h], yd_r.at[j, h])
            wait(rf.at[j, h], yf_r.at[j, h])
            total = pair_sum(3, j, h) + rd[j, h].astype(F32) + rf[j, h]
            t[j, h] = total.T.astype(BF16).reshape(ZL, 16, 128)
            xx = lax.rem(x + j, XS)

            def send_tile(i, carry, j=j, h=h, xx=xx):
                zz = lax.rem(zl + off8(i), ZL)
                send(t.at[j, h, zz], r.at[me], r_s, r_r, at(xx * ZL + zz, y, halves[h], c))
                return carry

            here = j == 0 and h == 1
            lax.fori_loop(0, 7 if here else 8, send_tile, 0)
            if here:
                pltpu.make_async_copy(t.at[0, 1, zl], r.at[me], r_r).start()

    def send_decay(i, carry):
        q = lax.rem(lay + i, LAYERS)
        send(dk.at[lax.div(q, ZL)], dks.at[lay], dk_s, dk_r, at(q, y, zh, c))
        return carry

    wait(pr.at[0], pair_r.at[0])
    send_far(0)
    wait(pr.at[1], pair_r.at[1])
    wait(pr.at[2], pair_r.at[2])
    send_first(0)
    send_far(1)
    pl.semaphore_wait(round_s.at[1], 2)
    signal(round_s.at[2], along_z(4))
    signal(round_s.at[2], along_z(-4))
    send_second(0)
    send_first(1)
    send_far(2)
    pl.semaphore_wait(round_s.at[2], 2)
    for step in range(1, XS):
        signal(round_s.at[3], along_x(step))
    send_second(1)
    send_first(2)
    send_far(3)
    pl.semaphore_wait(round_s.at[3], XS - 1)
    lax.fori_loop(1, LAYERS, send_decay, 0)
    pltpu.make_async_copy(dk.at[x], dks.at[lay], dk_r).start()
    wait(pr.at[3], pair_r.at[3])
    send_tiles(0)
    send_second(2)
    send_first(3)
    send_tiles(1)
    send_second(3)
    send_tiles(2)
    send_tiles(3)

    wait(dks, dk_r)
    rates = dks[:, 0, :]
    it[...] = jnp.concatenate([rates, jnp.zeros((128 - LAYERS, 128), F32)], axis=0).T
    mine = it[pl.ds(pl.multiple_of(zl * 16, 16), 16), :]
    for l in range(LAYERS):
        cpl[l] = mine[:, l : l + 1] * dks[l, 1:2, :]

    wait(r, r_r)
    state = None
    for l in reversed(range(LAYERS)):
        grad = r[l].astype(F32) + r[LAYERS + l].astype(F32)
        state = grad if state is None else grad + cpl[l] * state
        u[l] = state.astype(BF16)

    block = lax.div(z, 4)
    order = (0, 1, 3, 2)
    for d in order:

        def send_upper(i, carry, d=d):
            xx = lax.rem(x + lax.div(i + 1, 4), XS)
            zz = lax.rem(block + d, 4) * 4 + lax.rem(z + i + 1, 4)
            ll = xx * ZL + lax.rem(zz, ZL)
            send(u.at[ll], ul.at[z, x], u_s.at[d], u_r.at[(4 - d) % 4], at(ll, y, lax.div(zz, ZL), c))
            return carry

        lax.fori_loop(0, 15 if d == 0 else 16, send_upper, 0)
        if d == 0:
            pltpu.make_async_copy(u.at[lay], ul.at[z, x], u_r.at[0]).start()

    def rows_of(d, start=0, size=64):
        return pl.ds(pl.multiple_of(lax.rem(block + d, 4) * 64 + start, size), size)

    wait(si_v, ld_si)

    def side_s(d):
        rows = rows_of(d)
        places = pl.ds(lax.rem(block + d, 4) * 4, 4)
        wait(ul.at[places], u_r.at[d])
        upper = jnp.concatenate([ul[places, j].reshape(64, 128) for j in range(XS)], axis=1)
        sa[3, 1, rows] = jnp.dot(upper, si_v[...], preferred_element_type=F32).astype(BF16)
        src = sa.at[3, 1, rows]
        send(src, sa.at[1, 1, rows], sa_s, sa_r.at[0, d], near1)
        send(src, sa.at[2, 1, rows], sa_s, sa_r.at[1, d], near3)
        if d == order[3]:
            send(src, sa.at[0, 1, rows], sa_s, sa_r.at[2, d], near2)
        send(src, sa.at[3, 0, rows], sp_s, sp_r.at[3, d], partner)

    def pass_on(d):
        rows = rows_of(d)
        low, high = rows_of(d, 0, 32), rows_of(d, 32, 32)
        wait(sa.at[1, 1, rows], sa_r.at[0, d])
        if d != order[3]:
            send(sa.at[1, 1, low], sa.at[0, 1, low], sa_s, sa_r.at[2, d], near3)
        send(sa.at[1, 1, rows], sa.at[1, 0, rows], sp_s, sp_r.at[1, d], partner)
        wait(sa.at[2, 1, rows], sa_r.at[1, d])
        if d != order[3]:
            send(sa.at[2, 1, high], sa.at[0, 1, high], sa_s, sa_r.at[3, d], near1)
        send(sa.at[2, 1, rows], sa.at[2, 0, rows], sp_s, sp_r.at[2, d], partner)

    def opposite(d):
        rows = rows_of(d)
        if d == order[3]:
            wait(sa.at[0, 1, rows], sa_r.at[2, d])
        else:
            wait(sa.at[0, 1, rows_of(d, 0, 32)], sa_r.at[2, d])
            wait(sa.at[0, 1, rows_of(d, 32, 32)], sa_r.at[3, d])
        send(sa.at[0, 1, rows], sa.at[0, 0, rows], sp_s, sp_r.at[0, d], partner)

    d0, d1, d2, d3 = order
    side_s(d0)
    pass_on(d0)
    side_s(d1)
    opposite(d0)
    pass_on(d1)
    side_s(d2)
    opposite(d1)
    pass_on(d2)
    side_s(d3)
    opposite(d2)
    wait(ai_v, ld_ai)
    acc = jnp.dot(ai_v[3, 1], sa[3, 1], preferred_element_type=F32)
    pass_on(d3)
    acc += jnp.dot(ai_v[1, 1], sa[1, 1], preferred_element_type=F32)
    opposite(d3)
    acc += jnp.dot(ai_v[2, 1], sa[2, 1], preferred_element_type=F32)
    acc += jnp.dot(ai_v[0, 1], sa[0, 1], preferred_element_type=F32)
    for k in (3, 1, 2, 0):
        for d in range(4):
            wait(sa.at[k, 0, rows_of(d)], sp_r.at[k, d])
        acc += jnp.dot(ai_v[k, 0], sa[k, 0], preferred_element_type=F32)

    for j in range(4):
        xs[j] = acc[:, j * 128 : (j + 1) * 128].astype(BF16).reshape(ZL, 16, 128)
    for j in range(4):
        xx = lax.rem(x + j, XS)

        def send_solved(i, carry, xx=xx):
            zz = lax.rem(zl + off8(i), ZL)
            send(xs.at[xx, zz], rx.at[lay], x_s, x_r, at(xx * ZL + zz, y, zh, c))
            return carry

        lax.fori_loop(0, 7 if j == 0 else 8, send_solved, 0)
    pltpu.make_async_copy(xs.at[x, zl], rx.at[lay], x_r).start()

    wait(rx, x_r)
    state = None
    for l in range(LAYERS):
        solved = rx[l].astype(F32)
        state = solved if state is None else solved + cpl[l - 1] * state
        dd[l] = state.astype(BF16)

    for j in range(4):
        xx = lax.rem(x + j, XS)

        def send_lower(i, carry, xx=xx):
            zz = lax.rem(zl + off8(i), ZL)
            ll = xx * ZL + zz
            send(dd.at[ll], ot.at[zl, x], d_s, d_r, at(ll, y, zh, c))
            return carry

        lax.fori_loop(0, 7 if j == 0 else 8, send_lower, 0)
    pltpu.make_async_copy(dd.at[lay], ot.at[zl, x], d_r).start()

    wait(ot, d_r)
    for j in range(XS):
        out[0, :, j * 128 : (j + 1) * 128] = ot[:, j].reshape(ROWS, 128)

    wait(pr, pair_s)
    wait(so, y_s)
    wait(sd, y_s)
    wait(sf, y_s)
    wait(dks.at[pl.ds(0, LAYERS - 1)], dk_s)
    wait(r.at[pl.ds(0, 2 * LAYERS - 1)], r_s)
    for d in order:
        wait(u.at[pl.ds(0, 15 if d == 0 else 16)], u_s.at[d])
    wait(sa.at[pl.ds(0, 1), 0], sa_s)
    wait(sa.at[pl.ds(0, 1), 0], sa_s)
    wait(sa.at[pl.ds(0, 1), 0], sa_s)
    wait(sa.at[:, 0], sp_s)
    wait(rx.at[pl.ds(0, LAYERS - 1)], x_s)
    wait(rx.at[pl.ds(0, LAYERS - 1)], d_s)


def shards(activations, out_grads, a_inverse, s_inverse, in_decay, out_decay):
    vm = pltpu.VMEM
    dma = pltpu.SemaphoreType.DMA
    outside = pl.BlockSpec(memory_space=pltpu.HBM)
    inside = pl.BlockSpec(memory_space=pltpu.VMEM)
    unit = (4, 2, 128, 128)
    scratch = [
        vm((TOK, DIN), BF16),
        vm((TOK, DOUT), BF16),
        vm((DOUT, TOK), BF16),
        vm((4, 2, ROWS, 256), BF16),
        vm((DOUT, DOUT), BF16),
        vm((1, ROWS), F32),
        vm((1, DOUT), F32),
        vm((2, 4, 4, 2, 128, 128), F32),
        vm((4, 4, 2, 128, 128), F32),
        vm(unit, BF16), vm(unit, BF16), vm(unit, F32),
        vm(unit, BF16), vm(unit, BF16), vm(unit, F32),
        vm((4, 2, ZL, 16, 128), BF16),
        vm((2 * LAYERS, 16, 128), BF16),
        vm((XS, 2, 128), F32),
        vm((LAYERS, 2, 128), F32),
        vm((128, 128), F32),
        vm((LAYERS, 16, 128), F32),
        vm((LAYERS, 16, 128), BF16),
        vm((ZS, XS, 16, 128), BF16),
        vm((4, 2, 256, DOUT), BF16),
        vm((4, ZL, 16, 128), BF16),
        vm((LAYERS, 16, 128), BF16),
        vm((LAYERS, 16, 128), BF16),
        vm((ZL, XS, 16, 128), BF16),
        dma(()), dma(()), dma(()), dma(()), dma((2,)),
        pltpu.SemaphoreType.REGULAR((4,)),
        dma(()), dma((4,)),
        dma(()), dma((4, 2)), dma((4, 2)), dma((4, 2)),
        dma(()), dma(()),
        dma(()), dma(()),
        dma((4,)), dma((4,)),
        dma(()), dma((4, 4)),
        dma(()), dma((4, 4)),
        dma(()), dma(()),
        dma(()), dma(()),
    ]
    return pl.pallas_call(
        kernel,
        out_shape=jax.ShapeDtypeStruct((1, ROWS, DOUT), BF16),
        in_specs=[outside] * 6,
        out_specs=inside,
        scratch_shapes=scratch,
        compiler_params=pltpu.CompilerParams(
            collective_id=0, has_side_effects=True, vmem_limit_bytes=67043328
        ),
    )(activations, out_grads, a_inverse, s_inverse, in_decay, out_decay)


def solution(mesh):
    placed = (
        P("layer", "dp", None),
        P("layer", "dp", None),
        P("layer", "dp", None),
        P("layer", None, None),
        P("layer", "dp"),
        P("layer", None),
    )
    return jax.shard_map(
        shards, mesh=mesh, in_specs=placed, out_specs=P("layer", "dp", None), check_vma=False
    )
```
